32 devices in a mesh: groups: 2 (over y), win: 4 (over z), head: 2 (over x), sub: 2 (over core).
Axes of the slice: x: 2, y: 2, z: 4, core: 2. Of those that a mesh axis runs over, the one named last changes fastest.
Arguments:
- queries: float32 [2048, 6144], P(('groups', 'win'), ('head', 'sub')), parts along dimension 0, may hold values from -6.5 to 6.5
- key_rows: float32 [2048, 6144], P(('groups', 'win'), ('head', 'sub')), parts along dimension 0, may hold values from -6.5 to 6.5
- value_rows: float32 [2048, 6144], P(('groups', 'win'), ('head', 'sub')), parts along dimension 0, may hold values from -6 to 6
- merge_target: int32 [2048], P(('groups', 'win')), parts along dimension 0, may hold values from 0 to 831, as said below
Outputs:
- attended: float32 [2048, 6144], P(('groups', 'win'), ('head', 'sub')), parts along dimension 0
The draws below stay inside these ranges and needn't reach their ends.
There are 2 independent parts, one for each index of `groups`. The reference program is written for one: setup_inputs(seed, part) draws one part's arguments, and reference() takes and returns one part's arrays. A program takes and returns all parts, laid end to end along the dimension named above; each array names one. Nothing has to cross between parts.
Inputs may be any that keep to these rules, and one draw needn't show every extreme that they name: merge_target[r] lies in window merge_target[r] // 208; every merged row is joined by one or more rows; of the rows of one window, at most 64 join merged rows of any one window, exactly 64 join those of some window, and at least 52 join those of every window.
All inputs are finite; a program needn't handle non-finite values.
Results may differ from the reference program's by a relative error of at most 0.0003.
Values sent between devices are 32-bit elements; how exact they have to be, the bound alone decides.
No kernel may reach another device: no remote copies, remote signals or barrier semaphores. Data moves between devices by JAX's collectives and lax.ppermute only.
A program may use at most 64 MiB of HBM per device.

```python
import jax
import jax.numpy as jnp
from jax import lax

HEADS = 48
HEAD_DIM = 128
ROWS_PER_WINDOW = 256
WINDOW_TOTAL = 4
MERGED_WINDOW_ROWS = 208
DIM = 6144
ROWS = 1024


def draw_merge_target(key, part):
    base_key = jax.random.fold_in(key, 31)
    perm_key, order_key, offset_key, loose_key = jax.random.split(base_key, 4)
    block_rows = MERGED_WINDOW_ROWS // WINDOW_TOTAL
    spill_rows = (ROWS_PER_WINDOW - MERGED_WINDOW_ROWS) // 4
    role_index = jax.vmap(lambda subkey: jax.random.permutation(subkey, ROWS_PER_WINDOW))(jax.random.split(perm_key, WINDOW_TOTAL)).astype(jnp.int32)
    merged_order = jax.vmap(lambda subkey: jax.random.permutation(subkey, MERGED_WINDOW_ROWS))(jax.random.split(order_key, WINDOW_TOTAL)).astype(jnp.int32)
    shifted_window = jax.random.randint(offset_key, (WINDOW_TOTAL, 1), 1, WINDOW_TOTAL).astype(jnp.int32)
    loose_rows = jax.random.randint(loose_key, (WINDOW_TOTAL, ROWS_PER_WINDOW), 0, MERGED_WINDOW_ROWS).astype(jnp.int32)
    current_window = jnp.arange(WINDOW_TOTAL, dtype=jnp.int32)[:, None]
    band_index = role_index // block_rows
    anchor_win = (current_window - band_index) % WINDOW_TOTAL
    anchor_place = jnp.minimum(role_index, MERGED_WINDOW_ROWS - 1)
    surplus_rank = role_index - MERGED_WINDOW_ROWS
    scatter_window = (current_window + shifted_window + 1 + jnp.maximum(surplus_rank - spill_rows, 0) % (WINDOW_TOTAL - 1)) % WINDOW_TOTAL
    surplus_window = jnp.where(surplus_rank < spill_rows, (current_window + shifted_window) % WINDOW_TOTAL, scatter_window)
    is_anchor = role_index < MERGED_WINDOW_ROWS
    target_win = jnp.where(is_anchor, anchor_win, surplus_window)
    anchor_row = merged_order[anchor_win, anchor_place]
    target_row = jnp.where(is_anchor, anchor_row, loose_rows)
    return (target_win * MERGED_WINDOW_ROWS + target_row).reshape(-1).astype(jnp.int32)


def draw_queries(key, part):
    drawn_key = jax.random.fold_in(key, 41)
    result = jnp.clip(1.8 * jax.random.normal(drawn_key, (ROWS, DIM), jnp.float32), -6.5, 6.5)
    return result


def draw_key_rows(key, part):
    drawn_key = jax.random.fold_in(key, 43)
    result = jnp.clip(1.8 * jax.random.normal(drawn_key, (ROWS, DIM), jnp.float32), -6.5, 6.5)
    return result


def steps_of(key, shape, cuts, smallest, largest):
    def one(dim, blocks):
        draws = jax.random.uniform(jax.random.fold_in(jax.random.fold_in(key, 6), dim), (blocks,), jnp.float32, smallest / len(cuts), largest / len(cuts))
        return jnp.repeat(jnp.exp(draws), shape[dim] // blocks).reshape((-1,) + (1,) * (len(shape) - dim - 1))

    loudness = one(*cuts[0])
    for cut in cuts[1:]:
        loudness = loudness * one(*cut)
    return loudness


def bell_draw(stream_key, shape, scale, bound, shards=(), held_as=jnp.bfloat16):
    values = jax.random.normal(stream_key, shape, jnp.float32) * scale
    if len(shards) > 0:
        values = steps_of(stream_key, shape, shards, -0.22, 0.18) * values
    return jnp.clip(values, min=-bound, max=bound).astype(held_as)


def setup_inputs(seed: int = 0, part: int = 0) -> dict:
    splits = jax.random.split(jax.random.key(seed), 5)
    own_keys = jax.random.split(jax.random.fold_in(splits[4], part), 5)
    return {
        "queries": draw_queries(jax.random.fold_in(jax.random.fold_in(splits[4], part), 71), part),
        "key_rows": draw_key_rows(jax.random.fold_in(jax.random.fold_in(splits[4], part), 71), part),
        "value_rows": bell_draw(own_keys[2], (ROWS, DIM), 1.0, 6.0, ((0, 4), (1, 4)), jnp.float32),
        "merge_target": draw_merge_target(jax.random.fold_in(jax.random.fold_in(splits[4], part), 71), part),
    }


def reference(queries, key_rows, value_rows, merge_target):
    merged_total = WINDOW_TOTAL * MERGED_WINDOW_ROWS
    counts = jax.ops.segment_sum(jnp.ones((ROWS,), jnp.float32), merge_target, merged_total)

    def merge_rows(source):
        return jax.ops.segment_sum(source, merge_target, merged_total) / counts[:, None]

    merged_queries = merge_rows(queries)
    merged_keys = merge_rows(key_rows)
    merged_values = merge_rows(value_rows)
    scaling = 1.0 / (HEAD_DIM ** 0.5)

    def one_head(head_index):
        column = (head_index * HEAD_DIM).astype(jnp.int32)
        query_head = lax.dynamic_slice_in_dim(merged_queries, column, HEAD_DIM, 1)
        key_head = lax.dynamic_slice_in_dim(merged_keys, column, HEAD_DIM, 1)
        value_head = lax.dynamic_slice_in_dim(merged_values, column, HEAD_DIM, 1)

        def one_window(window_index):
            first = (window_index * MERGED_WINDOW_ROWS).astype(jnp.int32)
            query_block = lax.dynamic_slice_in_dim(query_head, first, MERGED_WINDOW_ROWS, 0)
            scores = jnp.dot(query_block, key_head.T, precision=lax.Precision.HIGHEST) * scaling
            top_score = jnp.max(scores, axis=1, keepdims=True)
            attention_weight = jnp.exp(scores - top_score)
            mixed = jnp.dot(attention_weight, value_head, precision=lax.Precision.HIGHEST)
            return mixed / jnp.sum(attention_weight, axis=1, keepdims=True)

        return lax.map(one_window, jnp.arange(WINDOW_TOTAL, dtype=jnp.int32)).reshape(merged_total, HEAD_DIM)

    per_head = lax.map(one_head, jnp.arange(HEADS, dtype=jnp.int32))
    merged_output = jnp.transpose(per_head, (1, 0, 2)).reshape(merged_total, DIM)
    return merged_output[merge_target]
```

```python
import functools
import math

import jax
import jax.numpy as jnp
from jax import lax
from jax.experimental import pallas as pl
from jax.experimental.pallas import tpu as pltpu
from jax.sharding import PartitionSpec as P

HEAD_DIM = 128
ROWS_PER_WINDOW = 256
MERGED_WINDOW_ROWS = 208


def slot_layout(merge_target, window_count, capacity):
    target_window = merge_target // MERGED_WINDOW_ROWS
    target_place = merge_target % MERGED_WINDOW_ROWS
    member = (target_window[:, None] == jnp.arange(window_count, dtype=jnp.int32)[None, :]).astype(
        jnp.int32
    )
    earlier = jnp.cumsum(member, axis=0) - member
    position = jnp.sum(earlier * member, axis=1)
    slot_index = target_window * capacity + position
    slot_total = window_count * capacity
    row_count = merge_target.shape[0]
    source_row = (
        jnp.full((slot_total,), row_count, jnp.int32)
        .at[slot_index]
        .set(jnp.arange(row_count, dtype=jnp.int32))
    )
    labels_flat = (
        jnp.zeros((slot_total,), jnp.float32)
        .at[slot_index]
        .set((target_place + 1).astype(jnp.float32))
    )
    return (slot_index, source_row, labels_flat.reshape(window_count, capacity))


def pack_rows(source, source_row, window_count, capacity):
    padding = jnp.zeros((1, source.shape[1]), source.dtype)
    return jnp.concatenate([source, padding], 0)[source_row].reshape(
        window_count, capacity, source.shape[1]
    )


def slot_counts(labels):
    label_index = labels.reshape(-1).astype(jnp.int32) - 1
    segment = jnp.where(label_index < 0, MERGED_WINDOW_ROWS, label_index)
    counts = jax.ops.segment_sum(
        jnp.ones(segment.shape, jnp.float32), segment, MERGED_WINDOW_ROWS + 1
    )[:MERGED_WINDOW_ROWS]
    return (segment, counts)


def average_slots(received, segment, counts):
    flattened = received.reshape(-1, received.shape[-1])
    totals = jax.ops.segment_sum(flattened, segment, MERGED_WINDOW_ROWS + 1)[:MERGED_WINDOW_ROWS]
    return totals / counts[:, None]


def by_windows(queries, key_rows, value_rows, merge_target):
    window_count = lax.axis_size("win")
    capacity = MERGED_WINDOW_ROWS // window_count + (ROWS_PER_WINDOW - MERGED_WINDOW_ROWS) // 4
    col_width = queries.shape[1]
    head_count = col_width // HEAD_DIM
    slot_index, source_row, labels = slot_layout(merge_target, window_count, capacity)
    pair_rows = jnp.concatenate([key_rows, value_rows], 1)
    packed_pair = pack_rows(pair_rows, source_row, window_count, capacity)
    received_pair, got_labels = (
        lax.all_to_all(packed_pair, "win", split_axis=0, concat_axis=0, tiled=True),
        lax.all_to_all(labels, "win", split_axis=0, concat_axis=0, tiled=True),
    )
    segment, counts = slot_counts(got_labels)
    merged_pair = average_slots(received_pair, segment, counts)
    merged_keys = merged_pair[:, :col_width]
    merged_values = merged_pair[:, col_width:]
    packed_queries = pack_rows(queries, source_row, window_count, capacity)
    received_queries = lax.all_to_all(
        packed_queries, "win", split_axis=0, concat_axis=0, tiled=True
    )
    merged_queries = average_slots(received_queries, segment, counts)
    scaling = 1.0 / math.sqrt(HEAD_DIM)
    query_head_stack = merged_queries.reshape(MERGED_WINDOW_ROWS, head_count, HEAD_DIM)
    running_max = jnp.full((head_count, MERGED_WINDOW_ROWS), -1e30, jnp.float32)
    portion_keys = lax.all_gather(merged_keys, "win", axis=0, tiled=True)
    portion_values = lax.all_gather(merged_values, "win", axis=0, tiled=True)
    key_head_stack = portion_keys.reshape(-1, head_count, HEAD_DIM)
    value_head_stack = portion_values.reshape(-1, head_count, HEAD_DIM)
    scores = (
        jnp.einsum(
            "frk,grk->rfg", query_head_stack, key_head_stack, precision=lax.Precision.HIGHEST
        )
        * scaling
    )
    new_max = jnp.maximum(running_max, jnp.max(scores, axis=2))
    attention_weight = jnp.exp(scores - new_max[:, :, None])
    new_sum = jnp.sum(attention_weight, axis=2)
    appended_rows = jnp.einsum(
        "tak,ktl->atl", attention_weight, value_head_stack, precision=lax.Precision.HIGHEST
    )
    merged_output = (appended_rows / jnp.transpose(new_sum)[:, :, None]).reshape(
        MERGED_WINDOW_ROWS, col_width
    )
    padded_output = jnp.concatenate([merged_output, jnp.zeros((1, col_width), jnp.float32)], 0)
    outgoing = padded_output[segment].reshape(window_count, capacity, col_width)
    returned = lax.all_to_all(outgoing, "win", split_axis=0, concat_axis=0, tiled=True)
    return returned.reshape(-1, col_width)[slot_index]


def split_terms(x):
    high = x.astype(jnp.bfloat16)
    low = (x - high.astype(jnp.float32)).astype(jnp.bfloat16)
    return high, low


def attend_kernel(
    peers, _, place_row_ref, place_col_ref, query_ref, key_ref, value_ref, *refs
):
    received, returned, own_ref = refs[:peers], refs[peers : 2 * peers], refs[2 * peers]
    rows_ref, query_cat, key_high, key_low, value_cat, output_cat = refs[2 * peers + 1 :]
    rows = query_ref.shape[0]
    row_total = rows * (peers + 1)
    merged_total = query_cat.shape[0]
    tile = MERGED_WINDOW_ROWS

    for part in range(3):
        for piece in range(peers + 1):
            if piece == 0:
                block = (query_ref, key_ref, value_ref)[part][...]
            else:
                block = received[piece - 1][part * rows : (part + 1) * rows, :]
            high, low = split_terms(block)
            span = slice(piece * rows, (piece + 1) * rows)
            rows_ref[span, 2 * part * HEAD_DIM : (2 * part + 1) * HEAD_DIM] = high
            rows_ref[span, (2 * part + 1) * HEAD_DIM : (2 * part + 2) * HEAD_DIM] = low

    scaling = math.log2(math.e) / math.sqrt(HEAD_DIM)
    place_row = place_row_ref[...]

    @pl.loop(0, merged_total // tile)
    def _(step):
        first = pl.multiple_of(step * tile, tile)
        merged_index = lax.broadcasted_iota(jnp.int32, (tile, row_total), 0) + first
        joins = merged_index == place_row
        counts = jnp.sum(joins.astype(jnp.float32), axis=1, keepdims=True)
        sums = jnp.dot(
            joins.astype(jnp.float32).astype(jnp.bfloat16),
            rows_ref[...],
            preferred_element_type=jnp.float32,
        )
        mean = [
            (sums[:, 2 * n * HEAD_DIM : (2 * n + 1) * HEAD_DIM]
             + sums[:, (2 * n + 1) * HEAD_DIM : (2 * n + 2) * HEAD_DIM]) / counts
            for n in range(3)
        ]
        span = pl.ds(first, tile)
        high, low = split_terms(mean[0] * scaling)
        query_cat[span, :] = jnp.concatenate([high, low], 1)
        high, low = split_terms(mean[1])
        key_high[span, :] = jnp.concatenate([high, high], 1)
        key_low[span, :] = jnp.concatenate([low, low], 1)
        high, low = split_terms(mean[2])
        value_cat[span, :] = jnp.concatenate([high, low], 1)

    contract = (((1,), (1,)), ((), ()))

    @pl.loop(0, merged_total // tile)
    def _(step):
        span = pl.ds(pl.multiple_of(step * tile, tile), tile)
        query = query_cat[span, :]
        scores = lax.dot_general(
            query, key_high[...], contract, preferred_element_type=jnp.float32
        ) + lax.dot_general(
            query, key_low[...], contract, preferred_element_type=jnp.float32
        )
        top = jnp.max(scores, axis=1, keepdims=True)
        weight = jnp.exp2(scores - top)
        total = jnp.sum(weight, axis=1, keepdims=True)
        high, low = split_terms(weight)
        mixed = jnp.dot(
            high, value_cat[...], preferred_element_type=jnp.float32
        ) + jnp.dot(low, value_cat[...], preferred_element_type=jnp.float32)
        output = (mixed[:, :HEAD_DIM] + mixed[:, HEAD_DIM:]) / total
        high, low = split_terms(output)
        output_cat[span, :] = jnp.concatenate([high, low], 1)

    for piece in range(peers, -1, -1):
        joined = lax.broadcasted_iota(jnp.int32, (rows, merged_total), 1) == (
            place_col_ref[piece * rows : (piece + 1) * rows, :]
        )
        both = jnp.dot(
            joined.astype(jnp.float32).astype(jnp.bfloat16),
            output_cat[...],
            preferred_element_type=jnp.float32,
        )
        out_ref = own_ref if piece == 0 else returned[piece - 1]
        out_ref[...] = both[:, :HEAD_DIM] + both[:, HEAD_DIM:]


def attend(own_head, place_row, place_col, queries, key_rows, value_rows, received):
    peers = len(received)
    rows = queries.shape[0]
    merged_total = (peers + 1) * MERGED_WINDOW_ROWS
    row_total = (peers + 1) * rows
    block = pl.BlockSpec((rows, HEAD_DIM), lambda i, head: (0, head[0]))
    whole = lambda shape: pl.BlockSpec(shape, lambda i, head: (0, 0))
    pairs = pltpu.VMEM((merged_total, 2 * HEAD_DIM), jnp.bfloat16)
    flops = 2 * merged_total * HEAD_DIM * (6 * row_total + 8 * merged_total + 2 * row_total)
    return pl.pallas_call(
        functools.partial(attend_kernel, peers),
        grid_spec=pltpu.PrefetchScalarGridSpec(
            num_scalar_prefetch=1,
            grid=(1,),
            in_specs=[whole(place_row.shape), whole(place_col.shape)]
            + [block] * 3
            + [whole((3 * rows, HEAD_DIM))] * peers,
            out_specs=[whole((rows, HEAD_DIM))] * (peers + 1),
            scratch_shapes=[pltpu.VMEM((row_total, 6 * HEAD_DIM), jnp.bfloat16)] + [pairs] * 5,
        ),
        out_shape=[jax.ShapeDtypeStruct((rows, HEAD_DIM), jnp.float32)] * (peers + 1),
        cost_estimate=pl.CostEstimate(
            flops=flops,
            transcendentals=merged_total * merged_total,
            bytes_accessed=4 * 4 * row_total * HEAD_DIM,
        ),
        name="attend",
    )(own_head, place_row, place_col, queries, key_rows, value_rows, *received)


def by_heads(queries, key_rows, value_rows, merge_target):
    window_count = lax.axis_size("win")
    rows, col_width = queries.shape
    per_window = col_width // HEAD_DIM // window_count
    window = lax.axis_index("win")
    flips = range(1, window_count)

    def swap(x, flip):
        return lax.ppermute(x, "win", [(n, n ^ flip) for n in range(window_count)])

    def columns(source, peer, head):
        return lax.dynamic_slice_in_dim(
            source, (peer * per_window + head) * HEAD_DIM, HEAD_DIM, 1
        )

    places = merge_target.astype(jnp.float32).reshape(rows // HEAD_DIM, HEAD_DIM)
    places = jnp.concatenate([places, jnp.zeros((8 - rows // HEAD_DIM, HEAD_DIM), jnp.float32)], 0)
    arrived = []
    for head in range(per_window):
        got = []
        for flip in flips:
            parts = [columns(s, window ^ flip, head) for s in (queries, key_rows, value_rows)]
            if head == 0:
                parts.append(places)
            got.append(swap(jnp.concatenate(parts, 0), flip))
        arrived.append(got)
    place = jnp.concatenate(
        [merge_target]
        + [got[3 * rows : 3 * rows + rows // HEAD_DIM].reshape(rows).astype(jnp.int32) for got in arrived[0]]
    )
    place_row, place_col = place[None, :], place[:, None]
    result = jnp.zeros((rows, col_width), jnp.float32)
    returned = []
    for head in range(per_window):
        own_head = (window * per_window + head).astype(jnp.int32)[None]
        *away, own = attend(
            own_head, place_row, place_col, queries, key_rows, value_rows, arrived[head]
        )
        returned.append((window, head, own))
        for flip, block in zip(flips, away):
            returned.append((window ^ flip, head, swap(block, flip)))
    for peer, head, block in returned:
        result = lax.dynamic_update_slice_in_dim(
            result, block, (peer * per_window + head) * HEAD_DIM, 1
        )
    return result


def local(queries, key_rows, value_rows, merge_target):
    window_count = lax.axis_size("win")
    head_count = queries.shape[1] // HEAD_DIM
    if head_count % window_count == 0 and window_count & (window_count - 1) == 0:
        return by_heads(queries, key_rows, value_rows, merge_target)
    return by_windows(queries, key_rows, value_rows, merge_target)


def solution(mesh):
    return jax.shard_map(
        local,
        mesh=mesh,
        in_specs=(
            P(("groups", "win"), ("head", "sub")),
            P(("groups", "win"), ("head", "sub")),
            P(("groups", "win"), ("head", "sub")),
            P(("groups", "win")),
        ),
        out_specs=P(("groups", "win"), ("head", "sub")),
        check_vma=False,
    )
```

```python
import functools
import math

import jax
import jax.numpy as jnp
from jax import lax
from jax.experimental import pallas as pl
from jax.experimental.pallas import tpu as pltpu
from jax.sharding import PartitionSpec as P


HEAD_DIM = 128
ROWS_PER_WINDOW = 256
MERGED_WINDOW_ROWS = 208


def slot_layout(merge_target, window_count, capacity):
    target_window = merge_target // MERGED_WINDOW_ROWS
    target_place = merge_target % MERGED_WINDOW_ROWS
    member = (target_window[:, None] == jnp.arange(window_count, dtype=jnp.int32)[None, :]).astype(
        jnp.int32
    )
    earlier = jnp.cumsum(member, axis=0) - member
    position = jnp.sum(earlier * member, axis=1)
    slot_index = target_window * capacity + position
    slot_total = window_count * capacity
    row_count = merge_target.shape[0]
    source_row = (
        jnp.full((slot_total,), row_count, jnp.int32)
        .at[slot_index]
        .set(jnp.arange(row_count, dtype=jnp.int32))
    )
    labels_flat = (
        jnp.zeros((slot_total,), jnp.float32)
        .at[slot_index]
        .set((target_place + 1).astype(jnp.float32))
    )
    return (slot_index, source_row, labels_flat.reshape(window_count, capacity))


def pack_rows(source, source_row, window_count, capacity):
    padding = jnp.zeros((1, source.shape[1]), source.dtype)
    return jnp.concatenate([source, padding], 0)[source_row].reshape(
        window_count, capacity, source.shape[1]
    )


def slot_counts(labels):
    label_index = labels.reshape(-1).astype(jnp.int32) - 1
    segment = jnp.where(label_index < 0, MERGED_WINDOW_ROWS, label_index)
    counts = jax.ops.segment_sum(
        jnp.ones(segment.shape, jnp.float32), segment, MERGED_WINDOW_ROWS + 1
    )[:MERGED_WINDOW_ROWS]
    return (segment, counts)


def average_slots(received, segment, counts):
    flattened = received.reshape(-1, received.shape[-1])
    totals = jax.ops.segment_sum(flattened, segment, MERGED_WINDOW_ROWS + 1)[:MERGED_WINDOW_ROWS]
    return totals / counts[:, None]


def by_windows(queries, key_rows, value_rows, merge_target):
    window_count = lax.axis_size("win")
    capacity = MERGED_WINDOW_ROWS // window_count + (ROWS_PER_WINDOW - MERGED_WINDOW_ROWS) // 4
    col_width = queries.shape[1]
    head_count = col_width // HEAD_DIM
    slot_index, source_row, labels = slot_layout(merge_target, window_count, capacity)
    pair_rows = jnp.concatenate([key_rows, value_rows], 1)
    packed_pair = pack_rows(pair_rows, source_row, window_count, capacity)
    received_pair, got_labels = (
        lax.all_to_all(packed_pair, "win", split_axis=0, concat_axis=0, tiled=True),
        lax.all_to_all(labels, "win", split_axis=0, concat_axis=0, tiled=True),
    )
    segment, counts = slot_counts(got_labels)
    merged_pair = average_slots(received_pair, segment, counts)
    merged_keys = merged_pair[:, :col_width]
    merged_values = merged_pair[:, col_width:]
    packed_queries = pack_rows(queries, source_row, window_count, capacity)
    received_queries = lax.all_to_all(
        packed_queries, "win", split_axis=0, concat_axis=0, tiled=True
    )
    merged_queries = average_slots(received_queries, segment, counts)
    scaling = 1.0 / math.sqrt(HEAD_DIM)
    query_head_stack = merged_queries.reshape(MERGED_WINDOW_ROWS, head_count, HEAD_DIM)
    running_max = jnp.full((head_count, MERGED_WINDOW_ROWS), -1e30, jnp.float32)
    portion_keys = lax.all_gather(merged_keys, "win", axis=0, tiled=True)
    portion_values = lax.all_gather(merged_values, "win", axis=0, tiled=True)
    key_head_stack = portion_keys.reshape(-1, head_count, HEAD_DIM)
    value_head_stack = portion_values.reshape(-1, head_count, HEAD_DIM)
    scores = (
        jnp.einsum(
            "frk,grk->rfg", query_head_stack, key_head_stack, precision=lax.Precision.HIGHEST
        )
        * scaling
    )
    new_max = jnp.maximum(running_max, jnp.max(scores, axis=2))
    attention_weight = jnp.exp(scores - new_max[:, :, None])
    new_sum = jnp.sum(attention_weight, axis=2)
    appended_rows = jnp.einsum(
        "tak,ktl->atl", attention_weight, value_head_stack, precision=lax.Precision.HIGHEST
    )
    merged_output = (appended_rows / jnp.transpose(new_sum)[:, :, None]).reshape(
        MERGED_WINDOW_ROWS, col_width
    )
    padded_output = jnp.concatenate([merged_output, jnp.zeros((1, col_width), jnp.float32)], 0)
    outgoing = padded_output[segment].reshape(window_count, capacity, col_width)
    returned = lax.all_to_all(outgoing, "win", split_axis=0, concat_axis=0, tiled=True)
    return returned.reshape(-1, col_width)[slot_index]


def split_terms(x):
    high = x.astype(jnp.bfloat16)
    low = (x - high.astype(jnp.float32)).astype(jnp.bfloat16)
    return high, low


def pack_kernel(flip, head, per_window, tailed, *refs):
    sources = refs[:3]
    packed_ref, landed = refs[3 + tailed], refs[4 + tailed]
    rows = sources[0].shape[0]
    peer = lax.axis_index("win") ^ flip
    first = pl.multiple_of((peer * per_window + head) * HEAD_DIM, HEAD_DIM)
    copies = [
        pltpu.make_async_copy(
            source.at[:, pl.ds(first, HEAD_DIM)],
            packed_ref.at[pl.ds(part * rows, rows), :],
            landed.at[part],
        )
        for part, source in enumerate(sources)
    ]
    if tailed:
        places_ref = refs[-1]
        copies.insert(0, pltpu.make_async_copy(refs[3], places_ref, landed.at[3]))
    for copy in copies:
        copy.start()
    for copy in copies:
        copy.wait()
    if tailed:
        lines = rows // HEAD_DIM
        packed_ref[3 * rows : 3 * rows + lines, :] = places_ref[...].astype(jnp.float32)
        packed_ref[3 * rows + lines :, :] = jnp.zeros((8 - lines, HEAD_DIM), jnp.float32)


def pack(sources, flip, head, per_window, places=None):
    rows = sources[0].shape[0]
    tailed = places is not None
    total = 3 * rows + 8 * tailed
    extra = [places] if tailed else []
    return pl.pallas_call(
        functools.partial(pack_kernel, flip, head, per_window, tailed),
        in_specs=[pl.BlockSpec(memory_space=pl.ANY)] * (3 + tailed),
        out_specs=pl.BlockSpec(memory_space=pltpu.VMEM),
        out_shape=jax.ShapeDtypeStruct((total, HEAD_DIM), jnp.float32),
        scratch_shapes=[pltpu.SemaphoreType.DMA((3 + tailed,))]
        + [pltpu.VMEM(p.shape, p.dtype) for p in extra],
        cost_estimate=pl.CostEstimate(
            flops=0, transcendentals=0, bytes_accessed=8 * total * HEAD_DIM
        ),
        name="pack",
    )(*sources, *extra)


def place_kernel(head, per_window, peers, *refs):
    blocks = refs[:len(peers)]
    result_ref, landed = refs[-2:]
    copies = []
    for n, (block, flip) in enumerate(zip(blocks, peers)):
        peer = lax.axis_index("win") ^ flip
        first = pl.multiple_of((peer * per_window + head[n]) * HEAD_DIM, HEAD_DIM)
        copies.append(
            pltpu.make_async_copy(block, result_ref.at[:, pl.ds(first, HEAD_DIM)], landed.at[n])
        )
    for copy in copies:
        copy.start()
    for copy in copies:
        copy.wait()


def put_blocks(entries, per_window, result_shape, result=None):
    blocks = [entry[2] for entry in entries]
    flips, heads = [entry[0] for entry in entries], [entry[1] for entry in entries]
    anywhere = pl.BlockSpec(memory_space=pl.ANY)
    extra = [] if result is None else [result]
    return pl.pallas_call(
        functools.partial(place_kernel, heads, per_window, flips),
        in_specs=[pl.BlockSpec(memory_space=pltpu.VMEM)] * len(blocks) + [anywhere] * len(extra),
        out_specs=anywhere,
        out_shape=result_shape,
        input_output_aliases={len(blocks): 0} if extra else {},
        scratch_shapes=[pltpu.SemaphoreType.DMA((len(blocks),))],
        cost_estimate=pl.CostEstimate(
            flops=0, transcendentals=0, bytes_accessed=8 * blocks[0].size * len(blocks)
        ),
        name="put_blocks",
    )(*blocks, *extra)


def attend_kernel(peers, place_row_ref, place_col_ref, *refs):
    received, returned = refs[:peers], refs[peers : 2 * peers]
    rows_ref, query_cat, key_high, key_low, value_cat, output_cat = refs[2 * peers :]
    rows = returned[0].shape[0]
    row_total = rows * peers
    merged_total = query_cat.shape[0]
    tile = MERGED_WINDOW_ROWS

    for part in range(3):
        for piece in range(peers):
            high, low = split_terms(received[piece][part * rows : (part + 1) * rows, :])
            span = slice(piece * rows, (piece + 1) * rows)
            rows_ref[span, 2 * part * HEAD_DIM : (2 * part + 1) * HEAD_DIM] = high
            rows_ref[span, (2 * part + 1) * HEAD_DIM : (2 * part + 2) * HEAD_DIM] = low

    scaling = math.log2(math.e) / math.sqrt(HEAD_DIM)
    place_row = place_row_ref[...]

    @pl.loop(0, merged_total // tile)
    def _(step):
        first = pl.multiple_of(step * tile, tile)
        merged_index = lax.broadcasted_iota(jnp.int32, (tile, row_total), 0) + first
        joins = merged_index == place_row
        counts = jnp.sum(joins.astype(jnp.float32), axis=1, keepdims=True)
        sums = jnp.dot(
            joins.astype(jnp.float32).astype(jnp.bfloat16),
            rows_ref[...],
            preferred_element_type=jnp.float32,
        )
        mean = [
            (sums[:, 2 * n * HEAD_DIM : (2 * n + 1) * HEAD_DIM]
             + sums[:, (2 * n + 1) * HEAD_DIM : (2 * n + 2) * HEAD_DIM]) / counts
            for n in range(3)
        ]
        span = pl.ds(first, tile)
        high, low = split_terms(mean[0] * scaling)
        query_cat[span, :] = jnp.concatenate([high, low], 1)
        high, low = split_terms(mean[1])
        key_high[span, :] = jnp.concatenate([high, high], 1)
        key_low[span, :] = jnp.concatenate([low, low], 1)
        high, low = split_terms(mean[2])
        value_cat[span, :] = jnp.concatenate([high, low], 1)

    contract = (((1,), (1,)), ((), ()))

    @pl.loop(0, merged_total // tile)
    def _(step):
        span = pl.ds(pl.multiple_of(step * tile, tile), tile)
        query = query_cat[span, :]
        scores = lax.dot_general(
            query, key_high[...], contract, preferred_element_type=jnp.float32
        ) + lax.dot_general(
            query, key_low[...], contract, preferred_element_type=jnp.float32
        )
        top = jnp.max(scores, axis=1, keepdims=True)
        weight = jnp.exp2(scores - top)
        total = jnp.sum(weight, axis=1, keepdims=True)
        high, low = split_terms(weight)
        mixed = jnp.dot(
            high, value_cat[...], preferred_element_type=jnp.float32
        ) + jnp.dot(low, value_cat[...], preferred_element_type=jnp.float32)
        output = (mixed[:, :HEAD_DIM] + mixed[:, HEAD_DIM:]) / total
        high, low = split_terms(output)
        output_cat[span, :] = jnp.concatenate([high, low], 1)

    for piece in range(peers):
        joined = lax.broadcasted_iota(jnp.int32, (rows, merged_total), 1) == (
            place_col_ref[piece * rows : (piece + 1) * rows, :]
        )
        both = jnp.dot(
            joined.astype(jnp.float32).astype(jnp.bfloat16),
            output_cat[...],
            preferred_element_type=jnp.float32,
        )
        returned[piece][...] = both[:, :HEAD_DIM] + both[:, HEAD_DIM:]


def attend(place_row, place_col, received):
    peers = len(received)
    rows = place_row.shape[1] // peers
    merged_total = peers * MERGED_WINDOW_ROWS
    row_total = peers * rows
    pairs = pltpu.VMEM((merged_total, 2 * HEAD_DIM), jnp.bfloat16)
    flops = 2 * merged_total * HEAD_DIM * (6 * row_total + 8 * merged_total + 2 * row_total)
    return pl.pallas_call(
        functools.partial(attend_kernel, peers),
        in_specs=[pl.BlockSpec(memory_space=pltpu.VMEM)] * (2 + peers),
        out_specs=[pl.BlockSpec(memory_space=pltpu.VMEM)] * peers,
        scratch_shapes=[pltpu.VMEM((row_total, 6 * HEAD_DIM), jnp.bfloat16)] + [pairs] * 5,
        out_shape=[jax.ShapeDtypeStruct((rows, HEAD_DIM), jnp.float32)] * peers,
        cost_estimate=pl.CostEstimate(
            flops=flops,
            transcendentals=merged_total * merged_total,
            bytes_accessed=4 * 4 * row_total * HEAD_DIM,
        ),
        name="attend",
    )(place_row, place_col, *received)


def by_heads(queries, key_rows, value_rows, merge_target):
    window_count = lax.axis_size("win")
    rows, col_width = queries.shape
    per_window = col_width // HEAD_DIM // window_count
    sources = (queries, key_rows, value_rows)
    flips = range(window_count - 1, 0, -1)

    def swap(x, flip):
        return lax.ppermute(x, "win", [(n, n ^ flip) for n in range(window_count)])

    lines = rows // HEAD_DIM
    arrived, own = [], []
    for head in range(per_window):
        got = []
        for flip in flips:
            places = merge_target.reshape(lines, HEAD_DIM) if head == 0 else None
            packed = pack(sources, flip, head, per_window, places)
            got.append(swap(packed, flip))
        arrived.append(got)
        own.append(pack(sources, 0, head, per_window))
    place = jnp.concatenate(
        [got[3 * rows : 3 * rows + lines].reshape(rows).astype(jnp.int32) for got in arrived[0]]
        + [merge_target]
    )
    place_row, place_col = place[None, :], place[:, None]
    result_shape = jax.ShapeDtypeStruct((rows, col_width), jnp.float32)
    early, late = [], []
    for head in range(per_window):
        blocks = attend(place_row, place_col, arrived[head] + [own[head]])
        early.append((0, head, blocks[-1]))
        for flip, block in zip(flips, blocks):
            (early if head < per_window - 1 else late).append((flip, head, swap(block, flip)))
    result = put_blocks(early, per_window, result_shape)
    window = lax.axis_index("win")
    for flip, head, block in (late[2], late[0], late[1]):
        result = lax.dynamic_update_slice_in_dim(
            result, block, ((window ^ flip) * per_window + head) * HEAD_DIM, 1
        )
    return result


def solution(mesh):
    spec = P(("groups", "win"), ("head", "sub"))
    window_count = mesh.shape["win"]

    def program(queries, key_rows, value_rows, merge_target):
        head_count = queries.shape[1] // HEAD_DIM // (mesh.shape["head"] * mesh.shape["sub"])
        spread = head_count % window_count == 0 and window_count & (window_count - 1) == 0

        def local(*args):
            if not spread:
                return by_windows(*args)
            return by_heads(*args)

        return jax.shard_map(
            local,
            mesh=mesh,
            in_specs=(spec, spec, spec, P(("groups", "win"))),
            out_specs=spec,
            check_vma=False,
        )(queries, key_rows, value_rows, merge_target)

    return program
```

```python
import functools
import math

import jax
import jax.numpy as jnp
from jax import lax
from jax.experimental import pallas as pl
from jax.experimental.pallas import tpu as pltpu
from jax.sharding import PartitionSpec as P


HEAD_DIM = 128
ROWS_PER_WINDOW = 256
MERGED_WINDOW_ROWS = 208


def slot_layout(merge_target, window_count, capacity):
    target_window = merge_target // MERGED_WINDOW_ROWS
    target_place = merge_target % MERGED_WINDOW_ROWS
    member = (target_window[:, None] == jnp.arange(window_count, dtype=jnp.int32)[None, :]).astype(
        jnp.int32
    )
    earlier = jnp.cumsum(member, axis=0) - member
    position = jnp.sum(earlier * member, axis=1)
    slot_index = target_window * capacity + position
    slot_total = window_count * capacity
    row_count = merge_target.shape[0]
    source_row = (
        jnp.full((slot_total,), row_count, jnp.int32)
        .at[slot_index]
        .set(jnp.arange(row_count, dtype=jnp.int32))
    )
    labels_flat = (
        jnp.zeros((slot_total,), jnp.float32)
        .at[slot_index]
        .set((target_place + 1).astype(jnp.float32))
    )
    return (slot_index, source_row, labels_flat.reshape(window_count, capacity))


def pack_rows(source, source_row, window_count, capacity):
    padding = jnp.zeros((1, source.shape[1]), source.dtype)
    return jnp.concatenate([source, padding], 0)[source_row].reshape(
        window_count, capacity, source.shape[1]
    )


def slot_counts(labels):
    label_index = labels.reshape(-1).astype(jnp.int32) - 1
    segment = jnp.where(label_index < 0, MERGED_WINDOW_ROWS, label_index)
    counts = jax.ops.segment_sum(
        jnp.ones(segment.shape, jnp.float32), segment, MERGED_WINDOW_ROWS + 1
    )[:MERGED_WINDOW_ROWS]
    return (segment, counts)


def average_slots(received, segment, counts):
    flattened = received.reshape(-1, received.shape[-1])
    totals = jax.ops.segment_sum(flattened, segment, MERGED_WINDOW_ROWS + 1)[:MERGED_WINDOW_ROWS]
    return totals / counts[:, None]


def by_windows(queries, key_rows, value_rows, merge_target):
    window_count = lax.axis_size("win")
    capacity = MERGED_WINDOW_ROWS // window_count + (ROWS_PER_WINDOW - MERGED_WINDOW_ROWS) // 4
    col_width = queries.shape[1]
    head_count = col_width // HEAD_DIM
    slot_index, source_row, labels = slot_layout(merge_target, window_count, capacity)
    pair_rows = jnp.concatenate([key_rows, value_rows], 1)
    packed_pair = pack_rows(pair_rows, source_row, window_count, capacity)
    received_pair, got_labels = (
        lax.all_to_all(packed_pair, "win", split_axis=0, concat_axis=0, tiled=True),
        lax.all_to_all(labels, "win", split_axis=0, concat_axis=0, tiled=True),
    )
    segment, counts = slot_counts(got_labels)
    merged_pair = average_slots(received_pair, segment, counts)
    merged_keys = merged_pair[:, :col_width]
    merged_values = merged_pair[:, col_width:]
    packed_queries = pack_rows(queries, source_row, window_count, capacity)
    received_queries = lax.all_to_all(
        packed_queries, "win", split_axis=0, concat_axis=0, tiled=True
    )
    merged_queries = average_slots(received_queries, segment, counts)
    scaling = 1.0 / math.sqrt(HEAD_DIM)
    query_head_stack = merged_queries.reshape(MERGED_WINDOW_ROWS, head_count, HEAD_DIM)
    running_max = jnp.full((head_count, MERGED_WINDOW_ROWS), -1e30, jnp.float32)
    portion_keys = lax.all_gather(merged_keys, "win", axis=0, tiled=True)
    portion_values = lax.all_gather(merged_values, "win", axis=0, tiled=True)
    key_head_stack = portion_keys.reshape(-1, head_count, HEAD_DIM)
    value_head_stack = portion_values.reshape(-1, head_count, HEAD_DIM)
    scores = (
        jnp.einsum(
            "frk,grk->rfg", query_head_stack, key_head_stack, precision=lax.Precision.HIGHEST
        )
        * scaling
    )
    new_max = jnp.maximum(running_max, jnp.max(scores, axis=2))
    attention_weight = jnp.exp(scores - new_max[:, :, None])
    new_sum = jnp.sum(attention_weight, axis=2)
    appended_rows = jnp.einsum(
        "tak,ktl->atl", attention_weight, value_head_stack, precision=lax.Precision.HIGHEST
    )
    merged_output = (appended_rows / jnp.transpose(new_sum)[:, :, None]).reshape(
        MERGED_WINDOW_ROWS, col_width
    )
    padded_output = jnp.concatenate([merged_output, jnp.zeros((1, col_width), jnp.float32)], 0)
    outgoing = padded_output[segment].reshape(window_count, capacity, col_width)
    returned = lax.all_to_all(outgoing, "win", split_axis=0, concat_axis=0, tiled=True)
    return returned.reshape(-1, col_width)[slot_index]


def split_terms(x, count):
    terms = []
    for _ in range(count):
        terms.append(x.astype(jnp.bfloat16))
        x = x - terms[-1].astype(jnp.float32)
    return terms


TERMS = (3, 3, 2)


def pack_kernel(flip, head, per_window, tailed, *refs):
    sources = refs[:3]
    packed_ref, landed = refs[3 + tailed], refs[4 + tailed]
    rows = sources[0].shape[0]
    peer = lax.axis_index("win") ^ flip
    first = pl.multiple_of((peer * per_window + head) * HEAD_DIM, HEAD_DIM)
    copies = [
        pltpu.make_async_copy(
            source.at[:, pl.ds(first, HEAD_DIM)],
            packed_ref.at[pl.ds(part * rows, rows), :],
            landed.at[part],
        )
        for part, source in enumerate(sources)
    ]
    if tailed:
        places_ref = refs[-1]
        copies.insert(0, pltpu.make_async_copy(refs[3], places_ref, landed.at[3]))
    for copy in copies:
        copy.start()
    for copy in copies:
        copy.wait()
    if tailed:
        lines = rows // HEAD_DIM
        packed_ref[3 * rows : 3 * rows + lines, :] = places_ref[...].astype(jnp.float32)
        packed_ref[3 * rows + lines :, :] = jnp.zeros((8 - lines, HEAD_DIM), jnp.float32)


def pack(sources, flip, head, per_window, places=None):
    rows = sources[0].shape[0]
    tailed = places is not None
    total = 3 * rows + 8 * tailed
    extra = [places] if tailed else []
    return pl.pallas_call(
        functools.partial(pack_kernel, flip, head, per_window, tailed),
        in_specs=[pl.BlockSpec(memory_space=pl.ANY)] * (3 + tailed),
        out_specs=pl.BlockSpec(memory_space=pltpu.VMEM),
        out_shape=jax.ShapeDtypeStruct((total, HEAD_DIM), jnp.float32),
        scratch_shapes=[pltpu.SemaphoreType.DMA((3 + tailed,))]
        + [pltpu.VMEM(p.shape, p.dtype) for p in extra],
        cost_estimate=pl.CostEstimate(
            flops=0, transcendentals=0, bytes_accessed=8 * total * HEAD_DIM
        ),
        name="pack",
    )(*sources, *extra)


def place_kernel(head, per_window, peers, *refs):
    blocks = refs[:len(peers)]
    result_ref, landed = refs[-2:]
    copies = []
    for n, (block, flip) in enumerate(zip(blocks, peers)):
        peer = lax.axis_index("win") ^ flip
        first = pl.multiple_of((peer * per_window + head[n]) * HEAD_DIM, HEAD_DIM)
        copies.append(
            pltpu.make_async_copy(block, result_ref.at[:, pl.ds(first, HEAD_DIM)], landed.at[n])
        )
    for copy in copies:
        copy.start()
    for copy in copies:
        copy.wait()


def put_blocks(entries, per_window, result_shape, result=None):
    blocks = [entry[2] for entry in entries]
    flips, heads = [entry[0] for entry in entries], [entry[1] for entry in entries]
    anywhere = pl.BlockSpec(memory_space=pl.ANY)
    extra = [] if result is None else [result]
    return pl.pallas_call(
        functools.partial(place_kernel, heads, per_window, flips),
        in_specs=[pl.BlockSpec(memory_space=pltpu.VMEM)] * len(blocks) + [anywhere] * len(extra),
        out_specs=anywhere,
        out_shape=result_shape,
        input_output_aliases={len(blocks): 0} if extra else {},
        scratch_shapes=[pltpu.SemaphoreType.DMA((len(blocks),))],
        cost_estimate=pl.CostEstimate(
            flops=0, transcendentals=0, bytes_accessed=8 * blocks[0].size * len(blocks)
        ),
        name="put_blocks",
    )(*blocks, *extra)


def attend_kernel(peers, place_row_ref, place_col_ref, *refs):
    received, returned = refs[:peers], refs[peers : 2 * peers]
    rows_ref, query_main, query_rest, key_high, key_mid, key_rest, value_cat, output_cat = refs[
        2 * peers :
    ]
    rows = returned[0].shape[0]
    row_total = rows * peers
    merged_total = query_main.shape[0]
    tile = MERGED_WINDOW_ROWS

    for piece in range(peers):
        column = 0
        for part, count in enumerate(TERMS):
            block = received[piece][part * rows : (part + 1) * rows, :]
            for term in split_terms(block, count):
                rows_ref[piece * rows : (piece + 1) * rows, column : column + HEAD_DIM] = term
                column += HEAD_DIM

    scaling = math.log2(math.e) / math.sqrt(HEAD_DIM)
    place_row = place_row_ref[...]

    for first in range(0, merged_total, tile):
        merged_index = lax.broadcasted_iota(jnp.int32, (tile, row_total), 0) + first
        joins = (merged_index == place_row).astype(jnp.float32)
        counts = jnp.sum(joins, axis=1, keepdims=True)
        sums = jnp.dot(
            joins.astype(jnp.bfloat16), rows_ref[...], preferred_element_type=jnp.float32
        )
        means = []
        column = 0
        for count in TERMS:
            terms = [
                sums[:, column + n * HEAD_DIM : column + (n + 1) * HEAD_DIM] for n in range(count)
            ]
            means.append(sum(terms[-2::-1], terms[-1]) / counts)
            column += count * HEAD_DIM
        span = slice(first, first + tile)
        high, mid, low = split_terms(means[0] * scaling, 3)
        query_main[span, :] = jnp.concatenate([high, mid], 1)
        query_rest[span, :] = jnp.concatenate([high, low], 1)
        high, mid, low = split_terms(means[1], 3)
        key_high[span, :] = jnp.concatenate([high, high], 1)
        key_mid[span, :] = jnp.concatenate([mid, mid], 1)
        key_rest[span, :] = jnp.concatenate([low, high], 1)
        value_cat[span, :] = jnp.concatenate(split_terms(means[2], 2), 1)

    contract = (((1,), (1,)), ((), ()))

    for first in range(0, merged_total, tile):
        span = slice(first, first + tile)
        scores = 0.0
        for query, key in (
            (query_rest, key_rest),
            (query_main, key_mid),
            (query_main, key_high),
        ):
            scores += lax.dot_general(
                query[span, :], key[...], contract, preferred_element_type=jnp.float32
            )
        top = jnp.max(scores, axis=1, keepdims=True)
        weight = jnp.exp2(scores - top)
        total = jnp.sum(weight, axis=1, keepdims=True)
        high, low = split_terms(weight, 2)
        mixed = jnp.dot(
            high, value_cat[...], preferred_element_type=jnp.float32
        ) + jnp.dot(low, value_cat[...], preferred_element_type=jnp.float32)
        output = (mixed[:, :HEAD_DIM] + mixed[:, HEAD_DIM:]) / total
        output_cat[span, :] = jnp.concatenate(split_terms(output, 2), 1)

    for piece in range(peers):
        joined = lax.broadcasted_iota(jnp.int32, (rows, merged_total), 1) == (
            place_col_ref[piece * rows : (piece + 1) * rows, :]
        )
        both = jnp.dot(
            joined.astype(jnp.float32).astype(jnp.bfloat16),
            output_cat[...],
            preferred_element_type=jnp.float32,
        )
        returned[piece][...] = both[:, :HEAD_DIM] + both[:, HEAD_DIM:]


def attend(place_row, place_col, received):
    peers = len(received)
    rows = place_row.shape[1] // peers
    merged_total = peers * MERGED_WINDOW_ROWS
    row_total = peers * rows
    pairs = pltpu.VMEM((merged_total, 2 * HEAD_DIM), jnp.bfloat16)
    flops = 2 * merged_total * HEAD_DIM * (10 * row_total + 10 * merged_total)
    return pl.pallas_call(
        functools.partial(attend_kernel, peers),
        in_specs=[pl.BlockSpec(memory_space=pltpu.VMEM)] * (2 + peers),
        out_specs=[pl.BlockSpec(memory_space=pltpu.VMEM)] * peers,
        scratch_shapes=[pltpu.VMEM((row_total, sum(TERMS) * HEAD_DIM), jnp.bfloat16)] + [pairs] * 7,
        out_shape=[jax.ShapeDtypeStruct((rows, HEAD_DIM), jnp.float32)] * peers,
        cost_estimate=pl.CostEstimate(
            flops=flops,
            transcendentals=merged_total * merged_total,
            bytes_accessed=4 * 4 * row_total * HEAD_DIM,
        ),
        name="attend",
    )(place_row, place_col, *received)


def by_heads(queries, key_rows, value_rows, merge_target):
    window_count = lax.axis_size("win")
    rows, col_width = queries.shape
    per_window = col_width // HEAD_DIM // window_count
    sources = (queries, key_rows, value_rows)
    flips = range(window_count - 1, 0, -1)

    def swap(x, flip):
        return lax.ppermute(x, "win", [(n, n ^ flip) for n in range(window_count)])

    lines = rows // HEAD_DIM
    arrived, own = [], []
    for head in range(per_window):
        got = []
        for flip in flips:
            places = merge_target.reshape(lines, HEAD_DIM) if head == 0 else None
            packed = pack(sources, flip, head, per_window, places)
            got.append(swap(packed, flip))
        arrived.append(got)
        own.append(pack(sources, 0, head, per_window))
    place = jnp.concatenate(
        [got[3 * rows : 3 * rows + lines].reshape(rows).astype(jnp.int32) for got in arrived[0]]
        + [merge_target]
    )
    place_row, place_col = place[None, :], place[:, None]
    result_shape = jax.ShapeDtypeStruct((rows, col_width), jnp.float32)
    early, late = [], []
    for head in range(per_window):
        blocks = attend(place_row, place_col, arrived[head] + [own[head]])
        early.append((0, head, blocks[-1]))
        for flip, block in zip(flips, blocks):
            (early if head == 0 else late).append((flip, head, swap(block, flip)))
    result = put_blocks(early, per_window, result_shape)
    window = lax.axis_index("win")
    for flip, head, block in (*late[2:3], *late[1::-1], late[5], *late[3:5]):
        result = lax.dynamic_update_slice_in_dim(
            result, block, ((window ^ flip) * per_window + head) * HEAD_DIM, 1
        )
    return result


def solution(mesh):
    spec = P(("groups", "win"), ("head", "sub"))
    window_count = mesh.shape["win"]

    def program(queries, key_rows, value_rows, merge_target):
        head_count = queries.shape[1] // HEAD_DIM // (mesh.shape["head"] * mesh.shape["sub"])
        spread = head_count % window_count == 0 and window_count & (window_count - 1) == 0

        def local(*args):
            if not spread:
                return by_windows(*args)
            return by_heads(*args)

        return jax.shard_map(
            local,
            mesh=mesh,
            in_specs=(spec, spec, spec, P(("groups", "win"))),
            out_specs=spec,
            check_vma=False,
        )(queries, key_rows, value_rows, merge_target)

    return program
```

```python
import functools
import math

import jax
import jax.numpy as jnp
from jax import lax
from jax.experimental import pallas as pl
from jax.experimental.pallas import tpu as pltpu
from jax.sharding import PartitionSpec as P


HEAD_DIM = 128
ROWS_PER_WINDOW = 256
MERGED_WINDOW_ROWS = 208


def slot_layout(merge_target, window_count, capacity):
    target_window = merge_target // MERGED_WINDOW_ROWS
    target_place = merge_target % MERGED_WINDOW_ROWS
    member = (target_window[:, None] == jnp.arange(window_count, dtype=jnp.int32)[None, :]).astype(
        jnp.int32
    )
    earlier = jnp.cumsum(member, axis=0) - member
    position = jnp.sum(earlier * member, axis=1)
    slot_index = target_window * capacity + position
    slot_total = window_count * capacity
    row_count = merge_target.shape[0]
    source_row = (
        jnp.full((slot_total,), row_count, jnp.int32)
        .at[slot_index]
        .set(jnp.arange(row_count, dtype=jnp.int32))
    )
    labels_flat = (
        jnp.zeros((slot_total,), jnp.float32)
        .at[slot_index]
        .set((target_place + 1).astype(jnp.float32))
    )
    return (slot_index, source_row, labels_flat.reshape(window_count, capacity))


def pack_rows(source, source_row, window_count, capacity):
    padding = jnp.zeros((1, source.shape[1]), source.dtype)
    return jnp.concatenate([source, padding], 0)[source_row].reshape(
        window_count, capacity, source.shape[1]
    )


def slot_counts(labels):
    label_index = labels.reshape(-1).astype(jnp.int32) - 1
    segment = jnp.where(label_index < 0, MERGED_WINDOW_ROWS, label_index)
    counts = jax.ops.segment_sum(
        jnp.ones(segment.shape, jnp.float32), segment, MERGED_WINDOW_ROWS + 1
    )[:MERGED_WINDOW_ROWS]
    return (segment, counts)


def average_slots(received, segment, counts):
    flattened = received.reshape(-1, received.shape[-1])
    totals = jax.ops.segment_sum(flattened, segment, MERGED_WINDOW_ROWS + 1)[:MERGED_WINDOW_ROWS]
    return totals / counts[:, None]


def by_windows(queries, key_rows, value_rows, merge_target):
    window_count = lax.axis_size("win")
    capacity = MERGED_WINDOW_ROWS // window_count + (ROWS_PER_WINDOW - MERGED_WINDOW_ROWS) // 4
    col_width = queries.shape[1]
    head_count = col_width // HEAD_DIM
    slot_index, source_row, labels = slot_layout(merge_target, window_count, capacity)
    pair_rows = jnp.concatenate([key_rows, value_rows], 1)
    packed_pair = pack_rows(pair_rows, source_row, window_count, capacity)
    received_pair, got_labels = (
        lax.all_to_all(packed_pair, "win", split_axis=0, concat_axis=0, tiled=True),
        lax.all_to_all(labels, "win", split_axis=0, concat_axis=0, tiled=True),
    )
    segment, counts = slot_counts(got_labels)
    merged_pair = average_slots(received_pair, segment, counts)
    merged_keys = merged_pair[:, :col_width]
    merged_values = merged_pair[:, col_width:]
    packed_queries = pack_rows(queries, source_row, window_count, capacity)
    received_queries = lax.all_to_all(
        packed_queries, "win", split_axis=0, concat_axis=0, tiled=True
    )
    merged_queries = average_slots(received_queries, segment, counts)
    scaling = 1.0 / math.sqrt(HEAD_DIM)
    query_head_stack = merged_queries.reshape(MERGED_WINDOW_ROWS, head_count, HEAD_DIM)
    running_max = jnp.full((head_count, MERGED_WINDOW_ROWS), -1e30, jnp.float32)
    portion_keys = lax.all_gather(merged_keys, "win", axis=0, tiled=True)
    portion_values = lax.all_gather(merged_values, "win", axis=0, tiled=True)
    key_head_stack = portion_keys.reshape(-1, head_count, HEAD_DIM)
    value_head_stack = portion_values.reshape(-1, head_count, HEAD_DIM)
    scores = (
        jnp.einsum(
            "frk,grk->rfg", query_head_stack, key_head_stack, precision=lax.Precision.HIGHEST
        )
        * scaling
    )
    new_max = jnp.maximum(running_max, jnp.max(scores, axis=2))
    attention_weight = jnp.exp(scores - new_max[:, :, None])
    new_sum = jnp.sum(attention_weight, axis=2)
    appended_rows = jnp.einsum(
        "tak,ktl->atl", attention_weight, value_head_stack, precision=lax.Precision.HIGHEST
    )
    merged_output = (appended_rows / jnp.transpose(new_sum)[:, :, None]).reshape(
        MERGED_WINDOW_ROWS, col_width
    )
    padded_output = jnp.concatenate([merged_output, jnp.zeros((1, col_width), jnp.float32)], 0)
    outgoing = padded_output[segment].reshape(window_count, capacity, col_width)
    returned = lax.all_to_all(outgoing, "win", split_axis=0, concat_axis=0, tiled=True)
    return returned.reshape(-1, col_width)[slot_index]


TERMS = (3, 3, 2)


def split_terms(x, count):
    terms = []
    for _ in range(count):
        terms.append(x.astype(jnp.bfloat16))
        x = x - terms[-1].astype(jnp.float32)
    return terms


def pack_kernel(flip, head, per_window, tailed, *refs):
    sources = refs[:3]
    packed_ref, landed = refs[3 + tailed], refs[4 + tailed]
    rows = sources[0].shape[0]
    peer = lax.axis_index("win") ^ flip
    first = pl.multiple_of((peer * per_window + head) * HEAD_DIM, HEAD_DIM)
    copies = [
        pltpu.make_async_copy(
            source.at[:, pl.ds(first, HEAD_DIM)],
            packed_ref.at[pl.ds(part * rows, rows), :],
            landed.at[part],
        )
        for part, source in enumerate(sources)
    ]
    if tailed:
        places_ref = refs[-1]
        copies.insert(0, pltpu.make_async_copy(refs[3], places_ref, landed.at[3]))
    for copy in copies:
        copy.start()
    for copy in copies:
        copy.wait()
    if tailed:
        lines = rows // HEAD_DIM
        packed_ref[3 * rows : 3 * rows + lines, :] = places_ref[...].astype(jnp.float32)
        packed_ref[3 * rows + lines :, :] = jnp.zeros((8 - lines, HEAD_DIM), jnp.float32)


def pack(sources, flip, head, per_window, places=None):
    rows = sources[0].shape[0]
    tailed = places is not None
    total = 3 * rows + 8 * tailed
    extra = [places] if tailed else []
    return pl.pallas_call(
        functools.partial(pack_kernel, flip, head, per_window, tailed),
        in_specs=[pl.BlockSpec(memory_space=pl.ANY)] * (3 + tailed),
        out_specs=pl.BlockSpec(memory_space=pltpu.VMEM),
        out_shape=jax.ShapeDtypeStruct((total, HEAD_DIM), jnp.float32),
        scratch_shapes=[pltpu.SemaphoreType.DMA((3 + tailed,))]
        + [pltpu.VMEM(p.shape, p.dtype) for p in extra],
        cost_estimate=pl.CostEstimate(
            flops=0, transcendentals=0, bytes_accessed=8 * total * HEAD_DIM
        ),
        name="pack",
    )(*sources, *extra)


def put_kernel(spots, per_window, *refs):
    blocks, result_ref, landed = refs[: len(spots)], refs[-2], refs[-1]
    copies = []
    for n, (flip, head) in enumerate(spots):
        peer = lax.axis_index("win") ^ flip
        first = pl.multiple_of((peer * per_window + head) * HEAD_DIM, HEAD_DIM)
        copies.append(
            pltpu.make_async_copy(
                blocks[n], result_ref.at[:, pl.ds(first, HEAD_DIM)], landed.at[n]
            )
        )
    for copy in copies:
        copy.start()
    for copy in copies:
        copy.wait()


def put_blocks(entries, per_window, col_width):
    blocks = [block for _, _, block in entries]
    spots = [(flip, head) for flip, head, _ in entries]
    return pl.pallas_call(
        functools.partial(put_kernel, spots, per_window),
        in_specs=[pl.BlockSpec(memory_space=pltpu.VMEM)] * len(blocks),
        out_specs=pl.BlockSpec(memory_space=pl.ANY),
        out_shape=jax.ShapeDtypeStruct((blocks[0].shape[0], col_width), jnp.float32),
        scratch_shapes=[pltpu.SemaphoreType.DMA((len(blocks),))],
        cost_estimate=pl.CostEstimate(
            flops=0, transcendentals=0, bytes_accessed=8 * blocks[0].size * len(blocks)
        ),
        name="put_blocks",
    )(*blocks)


def attend_kernel(peers, place_row_ref, place_col_ref, *refs):
    received, returned = refs[:peers], refs[peers : 2 * peers]
    rows_ref, query_main, query_rest, key_high, key_mid, key_rest, value_cat, output_cat = refs[
        2 * peers :
    ]
    rows = returned[0].shape[0]
    row_total = rows * peers
    merged_total = query_main.shape[0]
    tile = MERGED_WINDOW_ROWS

    for piece in range(peers):
        column = 0
        for part, count in enumerate(TERMS):
            block = received[piece][part * rows : (part + 1) * rows, :]
            for term in split_terms(block, count):
                rows_ref[piece * rows : (piece + 1) * rows, column : column + HEAD_DIM] = term
                column += HEAD_DIM

    scaling = math.log2(math.e) / math.sqrt(HEAD_DIM)
    place_row = place_row_ref[...]

    for first in range(0, merged_total, tile):
        merged_index = lax.broadcasted_iota(jnp.int32, (tile, row_total), 0) + first
        joins = (merged_index == place_row).astype(jnp.float32)
        counts = jnp.sum(joins, axis=1, keepdims=True)
        sums = jnp.dot(
            joins.astype(jnp.bfloat16), rows_ref[...], preferred_element_type=jnp.float32
        )
        means = []
        column = 0
        for count in TERMS:
            terms = [
                sums[:, column + n * HEAD_DIM : column + (n + 1) * HEAD_DIM] for n in range(count)
            ]
            means.append(sum(terms[-2::-1], terms[-1]) / counts)
            column += count * HEAD_DIM
        span = slice(first, first + tile)
        high, mid, low = split_terms(means[0] * scaling, 3)
        query_main[span, :] = jnp.concatenate([high, mid], 1)
        query_rest[span, :] = jnp.concatenate([high, low], 1)
        high, mid, low = split_terms(means[1], 3)
        key_high[span, :] = jnp.concatenate([high, high], 1)
        key_mid[span, :] = jnp.concatenate([mid, mid], 1)
        key_rest[span, :] = jnp.concatenate([low, high], 1)
        value_cat[span, :] = jnp.concatenate(split_terms(means[2], 2), 1)

    contract = (((1,), (1,)), ((), ()))

    for first in range(0, merged_total, tile):
        span = slice(first, first + tile)
        scores = 0.0
        for query, key in (
            (query_rest, key_rest),
            (query_main, key_mid),
            (query_main, key_high),
        ):
            scores += lax.dot_general(
                query[span, :], key[...], contract, preferred_element_type=jnp.float32
            )
        top = jnp.max(scores, axis=1, keepdims=True)
        weight = jnp.exp2(scores - top)
        total = jnp.sum(weight, axis=1, keepdims=True)
        high, low = split_terms(weight, 2)
        mixed = jnp.dot(
            high, value_cat[...], preferred_element_type=jnp.float32
        ) + jnp.dot(low, value_cat[...], preferred_element_type=jnp.float32)
        output = (mixed[:, :HEAD_DIM] + mixed[:, HEAD_DIM:]) / total
        output_cat[span, :] = jnp.concatenate(split_terms(output, 2), 1)

    for piece in range(peers):
        joined = lax.broadcasted_iota(jnp.int32, (rows, merged_total), 1) == (
            place_col_ref[piece * rows : (piece + 1) * rows, :]
        )
        both = jnp.dot(
            joined.astype(jnp.float32).astype(jnp.bfloat16),
            output_cat[...],
            preferred_element_type=jnp.float32,
        )
        returned[piece][...] = both[:, :HEAD_DIM] + both[:, HEAD_DIM:]


def attend(place_row, place_col, received):
    peers = len(received)
    rows = place_row.shape[1] // peers
    merged_total = peers * MERGED_WINDOW_ROWS
    row_total = peers * rows
    pairs = pltpu.VMEM((merged_total, 2 * HEAD_DIM), jnp.bfloat16)
    flops = 2 * merged_total * HEAD_DIM * (10 * row_total + 10 * merged_total)
    return pl.pallas_call(
        functools.partial(attend_kernel, peers),
        in_specs=[pl.BlockSpec(memory_space=pltpu.VMEM)] * (2 + peers),
        out_specs=[pl.BlockSpec(memory_space=pltpu.VMEM)] * peers,
        scratch_shapes=[pltpu.VMEM((row_total, sum(TERMS) * HEAD_DIM), jnp.bfloat16)] + [pairs] * 7,
        out_shape=[jax.ShapeDtypeStruct((rows, HEAD_DIM), jnp.float32)] * peers,
        cost_estimate=pl.CostEstimate(
            flops=flops,
            transcendentals=merged_total * merged_total,
            bytes_accessed=4 * 4 * row_total * HEAD_DIM,
        ),
        name="attend",
    )(place_row, place_col, *received)


def by_heads(queries, key_rows, value_rows, merge_target):
    window_count = lax.axis_size("win")
    rows, col_width = queries.shape
    per_window = col_width // HEAD_DIM // window_count
    sources = (queries, key_rows, value_rows)
    flips = range(window_count - 1, 0, -1)

    def swap(x, flip):
        return lax.ppermute(x, "win", [(n, n ^ flip) for n in range(window_count)])

    lines = rows // HEAD_DIM
    arrived, own = [], []
    for head in range(per_window):
        got = []
        for flip in flips:
            places = merge_target.reshape(lines, HEAD_DIM) if head == 0 else None
            packed = pack(sources, flip, head, per_window, places)
            got.append(swap(packed, flip))
        arrived.append(got)
        own.append(pack(sources, 0, head, per_window))
    place = jnp.concatenate(
        [got[3 * rows : 3 * rows + lines].reshape(rows).astype(jnp.int32) for got in arrived[0]]
        + [merge_target]
    )
    place_row, place_col = place[None, :], place[:, None]
    early, late = [], []
    for head in range(per_window):
        blocks = attend(place_row, place_col, arrived[head] + [own[head]])
        early.append((0, head, blocks[-1]))
        for flip, block in zip(flips, blocks):
            (early if head == 0 else late).append((flip, head, swap(block, flip)))
    result = put_blocks(early, per_window, col_width)
    window = lax.axis_index("win")
    for flip, head, block in sorted(late, key=lambda entry: (entry[1], entry[0] > 1, -entry[0])):
        result = lax.dynamic_update_slice_in_dim(
            result, block, ((window ^ flip) * per_window + head) * HEAD_DIM, 1
        )
    return result


def solution(mesh):
    spec = P(("groups", "win"), ("head", "sub"))
    window_count = mesh.shape["win"]

    def program(queries, key_rows, value_rows, merge_target):
        head_count = queries.shape[1] // HEAD_DIM // (mesh.shape["head"] * mesh.shape["sub"])
        spread = head_count % window_count == 0 and window_count & (window_count - 1) == 0

        def local(*args):
            if not spread:
                return by_windows(*args)
            return by_heads(*args)

        return jax.shard_map(
            local,
            mesh=mesh,
            in_specs=(spec, spec, spec, P(("groups", "win"))),
            out_specs=spec,
            check_vma=False,
        )(queries, key_rows, value_rows, merge_target)

    return program
```
